32 devices in a mesh: groups: 2 (over y), cells: 4 (over z), obs: 2 (over x), mem: 2 (over core).
Axes of the slice: x: 2, y: 2, z: 4, core: 2. Of those that a mesh axis runs over, the one named last changes fastest.
Arguments:
- members: bfloat16 [64, 32768], P('mem', ('groups', 'cells', 'obs')), parts along dimension 1, may hold values from -4 to 4
- observed: float32 [16384], P(('groups', 'cells', 'obs')), parts along dimension 0, may hold values from -6 to 6
- obs_error: float32 [16384], P(('groups', 'cells', 'obs')), parts along dimension 0, may hold values from 0.25 to 2
- obs_cells: int32 [16384], P(('groups', 'cells', 'obs')), parts along dimension 0, may hold values from 0 to 2047
- perturbations: bfloat16 [16384, 64], P(('groups', 'cells', 'obs')), parts along dimension 0, may hold values from -5 to 5
- region_ids: int32 [64], P(('groups', 'cells', 'obs')), parts along dimension 0, may hold values from 0 to 3
Outputs:
- updated: bfloat16 [64, 32768], P('mem', ('groups', 'cells', 'obs')), parts along dimension 1
The draws below stay inside these ranges and needn't reach their ends.
There are 2 independent parts, one for each index of `groups`. The reference program is written for one: setup_inputs(seed, part) draws one part's arguments, and reference() takes and returns one part's arrays. A program takes and returns all parts, laid end to end along the dimension named above; each array names one. Nothing has to cross between parts.
Inputs may be any that keep to these rules, and one draw needn't show every extreme that they name: obs_cells[j] names a cell of section j // 1024, the cells s * 2048 to (s + 1) * 2048 - 1 forming section s. `region_ids`: block b holds the cells b * 512 to (b + 1) * 512 - 1.
All inputs are finite; a program needn't handle non-finite values.
Results may differ from the reference program's by a relative error of at most 0.006.
Values may be sent and summed in bfloat16 or wider, within the bound.
A program may use at most 64 MiB of HBM per device.

```python
import jax
import jax.numpy as jnp

NE = 64
CELL_DEV = 2048
OBS_DEV = 1024
BLOCK = 512
NLOC = 4
ITERS = 1
CELLS = 16384
NOBS = 8192
NBLK = 32


def draw_obs_error(key, part):
    position = jnp.arange(NOBS, dtype=jnp.float32) / NOBS
    trend = jnp.exp(-0.5 * jnp.log(3.0) * position)
    rough = jnp.exp(jax.random.uniform(key, (NOBS,), jnp.float32, jnp.log(0.5), jnp.log(2.0)))
    return (rough * trend).astype(jnp.float32)


def plant(drawn, key, least, largest):
    longest = drawn.shape.index(max(drawn.shape))
    spots = []
    for shift in (0, 1):
        where = [jax.random.randint(jax.random.fold_in(key, axis), (), 0, length) for axis, length in enumerate(drawn.shape)]
        where[longest] = (where[longest] + shift) % drawn.shape[longest]
        spots.append(tuple(where))
    return drawn.at[spots[0]].set(least).at[spots[1]].set(largest)


def level_of(own_key, dims, split, low, high):
    factor_of, own = 1.0, jax.random.fold_in(own_key, 6)
    for dim, shards_of in split:
        draws = jnp.exp(jax.random.uniform(jax.random.fold_in(own, dim), (shards_of,), jnp.float32, low / len(split), high / len(split)))
        factor_of = factor_of * jnp.repeat(draws, dims[dim] // shards_of).reshape([-1 if axis == dim else 1 for axis in range(len(dims))])
    return factor_of


def normal_values(key, dims, spread, bound, shards=(), held_as=jnp.bfloat16):
    drawn = spread * jax.random.normal(key, dims, jnp.float32)
    if shards:
        drawn = drawn * level_of(key, dims, shards, -0.22, 0.18)
    return jnp.clip(drawn, -bound, bound).astype(held_as)


def setup_inputs(seed: int = 0, part: int = 0) -> dict:
    streams_of = jax.random.split(jax.random.key(seed), 7)
    own_keys = jax.random.split(jax.random.fold_in(streams_of[6], part), 7)
    members = normal_values(own_keys[0], (NE, CELLS), 1.0, 4.0, ((0, 2), (1, 8)))
    observed = normal_values(own_keys[1], (NOBS,), 1.5, 6.0, ((0, 8),), jnp.float32)
    obs_error = draw_obs_error(jax.random.fold_in(jax.random.fold_in(streams_of[6], part), 71), part)
    obs_cells = plant(jax.random.randint(own_keys[3], (NOBS,), 0, CELL_DEV), jax.random.fold_in(own_keys[3], 1), 0, CELL_DEV - 1).astype(jnp.int32)
    perturbations = normal_values(own_keys[4], (NOBS, NE), 1.0, 5.0, ((0, 8),))
    region_ids = plant(jax.random.randint(own_keys[5], (NBLK,), 0, NLOC), jax.random.fold_in(own_keys[5], 1), 0, NLOC - 1).astype(jnp.int32)
    return dict(members=members, observed=observed, obs_error=obs_error, obs_cells=obs_cells, perturbations=perturbations, region_ids=region_ids)


def solve_regions(gram, cross, misfit):
    damping = NE - 1.0 + misfit / NE
    eye = jnp.eye(NE, dtype=gram.dtype)
    system = gram + damping[:, None, None] * eye[None, :, :]
    factor = jnp.linalg.cholesky(system)
    return jax.vmap(lambda fac, rhs: jax.scipy.linalg.cho_solve((fac, True), rhs))(factor, cross)

def reference(members, observed, obs_error, obs_cells, perturbations, region_ids):
    cell_index = jnp.arange(NOBS, dtype=jnp.int32) // OBS_DEV * CELL_DEV + obs_cells.astype(jnp.int32)
    cell_region = jnp.repeat(region_ids, BLOCK)
    obs_region = cell_region[cell_index]
    ensemble = members.T
    for step in range(ITERS):
        center = jnp.sum(ensemble.astype(jnp.float32), axis=1) / NE
        anomaly = (ensemble.astype(jnp.float32) - center[:, None]).astype(jnp.bfloat16)
        values = ensemble[cell_index].astype(jnp.float32)
        predicted = values + 0.2 * values * values * values
        pmean = jnp.sum(predicted, axis=1) / NE
        sens = ((predicted - pmean[:, None]) / obs_error[:, None]).astype(jnp.bfloat16)
        innov = (observed[:, None] - predicted) / obs_error[:, None] + perturbations.astype(jnp.float32)
        innov_b = innov.astype(jnp.bfloat16)
        joined = jnp.concatenate([sens, innov_b], axis=1)
        grams = []
        misfits = []
        for region in range(NLOC):
            inside = obs_region == region
            masked = jnp.where(inside[:, None], sens, jnp.zeros_like(sens))
            grams.append(jnp.dot(masked.T.astype(jnp.float32), joined.astype(jnp.float32), preferred_element_type=jnp.float32))
            misfits.append(jnp.sum(jnp.where(inside[:, None], innov * innov, jnp.float32(0.0))))
        stacked = jnp.stack(grams)
        misfit = jnp.stack(misfits)
        coeff = solve_regions(stacked[:, :, :NE], stacked[:, :, NE:], misfit).astype(jnp.bfloat16)
        delta = jnp.zeros(ensemble.shape, jnp.float32)
        for region in range(NLOC):
            product = jnp.dot(anomaly.astype(jnp.float32), coeff[region].astype(jnp.float32), preferred_element_type=jnp.float32)
            delta = delta + jnp.where((cell_region == region)[:, None], product, jnp.float32(0.0))
        ensemble = (ensemble.astype(jnp.float32) + delta).astype(jnp.bfloat16)
    return ensemble.T
```

```python
import functools

import jax
import jax.numpy as jnp
from jax import lax
from jax.experimental import pallas as pl
from jax.experimental.pallas import tpu as pltpu
from jax.sharding import PartitionSpec as P

BLOCK = 512
NLOC = 4
LANE = 128
MESH = pl.DeviceIdType.MESH


def gather_lanes(table, cells):
    rows, width = table.shape
    columns = []
    for start in range(0, cells.shape[1], LANE):
        index = cells[:, start : start + LANE]
        low = jnp.broadcast_to(index % LANE, (rows, LANE))
        high = jnp.broadcast_to(index // LANE, (rows, LANE))
        total = None
        for part in range(width // LANE):
            found = jnp.take_along_axis(
                table[:, part * LANE : (part + 1) * LANE], low, axis=1, mode="promise_in_bounds"
            )
            total = found if total is None else jnp.where(high == part, found, total)
        columns.append(total)
    return jnp.concatenate(columns, axis=1)


def eliminate(rows, ne):
    groups = len(rows)
    sub = lax.broadcasted_iota(jnp.int32, rows[0].shape, 0)
    for block in range(groups):
        base = block * 8
        cols = [
            [jnp.broadcast_to(rows[g][:, base + j : base + j + 1], rows[g].shape) for g in range(groups)]
            for j in range(8)
        ]
        for j in range(8):
            inv = 1.0 / cols[j][block][j : j + 1, :]
            here = sub == j
            for l in range(j + 1, 8):
                factor = cols[l][block][j : j + 1, :] * inv
                for g in range(groups):
                    new = cols[l][g] - cols[j][g] * factor
                    cols[l][g] = jnp.where(here, factor, new) if g == block else new
            pivot_row = rows[block][j : j + 1, :] * inv
            for g in range(groups):
                new = rows[g] - cols[j][g] * pivot_row
                rows[g] = jnp.where(here, pivot_row, new) if g == block else new
    return rows


def kernel(
    nz, nx, nm, region_ref, members_ref, observed_ref, error_ref, cells_ref, noise_ref, out_ref,
    vals, whole, mine, slots, coeff,
    v_send, v_recv, w_send, w_recv, g_send, g_recv, c_send, c_recv,
):
    z, x, m = lax.axis_index("cells"), lax.axis_index("obs"), lax.axis_index("mem")
    half = members_ref.shape[0]
    ne = half * nm
    nreg = NLOC // nm
    chips = nz * nx
    blocks = region_ref.shape[0]

    def chip(offset):
        return {"cells": lax.rem(z + offset // nx, nz), "obs": lax.rem(x + offset % nx, nx)}

    def core(offset):
        return {"mem": lax.rem(m + offset, nm)}

    barrier = pltpu.get_barrier_semaphore()
    for offset in range(1, nm):
        pl.semaphore_signal(barrier, inc=1, device_id=core(offset), device_id_type=MESH)
    for offset in range(1, chips):
        pl.semaphore_signal(barrier, inc=1, device_id=chip(offset), device_id_type=MESH)

    own = pl.ds(pl.multiple_of(m * half, half), half)
    cells = cells_ref[...]
    members = members_ref[...]
    vals[own, :] = gather_lanes(members.astype(jnp.float32), cells).astype(jnp.bfloat16)

    pl.semaphore_wait(barrier, nm - 1 + chips - 1)
    swaps = []
    for offset in range(1, nm):
        swaps.append(
            pltpu.make_async_remote_copy(
                src_ref=vals.at[own], dst_ref=vals.at[own],
                send_sem=v_send.at[offset - 1], recv_sem=v_recv.at[offset - 1],
                device_id=core(offset), device_id_type=MESH,
            )
        )
        swaps[-1].start()
    fetches = []
    for offset in range(1, nm):
        fetches.append(
            pltpu.make_async_remote_copy(
                src_ref=members_ref, dst_ref=whole.at[own],
                send_sem=w_send.at[offset - 1], recv_sem=w_recv.at[offset - 1],
                device_id=core(offset), device_id_type=MESH,
            )
        )
        fetches[-1].start()
    whole[own, :] = members

    eye = (
        lax.broadcasted_iota(jnp.int32, (ne, ne), 0) == lax.broadcasted_iota(jnp.int32, (ne, ne), 1)
    ).astype(jnp.float32).astype(jnp.bfloat16)
    noise = lax.dot_general(
        eye, noise_ref[...], (((1,), (1,)), ((), ())), preferred_element_type=jnp.float32
    )
    block_of = cells // BLOCK
    region = jnp.full(cells.shape, region_ref[0], jnp.int32)
    for b in range(1, blocks):
        region = jnp.where(block_of == b, region_ref[b], region)
    masks = [region == m * nreg + i for i in range(nreg)]
    error = error_ref[...]
    observed = observed_ref[...]

    for copy in swaps:
        copy.wait()
    values = vals[...].astype(jnp.float32)
    predicted = values + 0.2 * values * values * values
    pmean = jnp.sum(predicted, axis=0, keepdims=True) / ne
    inverse = 1.0 / error
    sens = (predicted - pmean) * inverse
    innov = (observed - predicted) * inverse + noise
    square = jnp.sum(innov * innov, axis=0, keepdims=True)
    joined = jnp.concatenate([sens, innov], axis=0).astype(jnp.bfloat16)
    masked = jnp.concatenate([jnp.where(mask, sens, 0.0) for mask in masks], axis=0).astype(jnp.bfloat16)
    partial = lax.dot_general(
        masked, joined, (((1,), (1,)), ((), ())), preferred_element_type=jnp.float32
    )
    diagonal = (
        lax.broadcasted_iota(jnp.int32, (ne, 2 * ne), 0)
        == lax.broadcasted_iota(jnp.int32, (ne, 2 * ne), 1)
    )
    partial = partial + jnp.concatenate(
        [
            jnp.where(
                diagonal,
                jnp.sum(jnp.where(mask, square, 0.0), axis=1, keepdims=True) / ne,
                0.0,
            )
            for mask in masks
        ],
        axis=0,
    )
    mine[...] = partial.astype(jnp.bfloat16)
    shares = []
    for offset in range(1, chips):
        shares.append(
            pltpu.make_async_remote_copy(
                src_ref=mine, dst_ref=slots.at[offset - 1],
                send_sem=g_send.at[offset - 1], recv_sem=g_recv.at[offset - 1],
                device_id=chip(offset), device_id_type=MESH,
            )
        )
        shares[-1].start()

    for copy in fetches:
        copy.wait()
    ensemble = whole[...].astype(jnp.float32)
    center = jnp.sum(ensemble, axis=0, keepdims=True) / ne
    anomaly = (ensemble - center).astype(jnp.bfloat16)

    total = mine[...].astype(jnp.float32)
    for offset, copy in enumerate(shares):
        copy.wait()
        total = total + slots[offset].astype(jnp.float32)

    damping = jnp.where(diagonal, ne - 1.0, 0.0)
    solved = []
    for i in range(nreg):
        system = total[i * ne : (i + 1) * ne] + damping
        rows = eliminate([system[g : g + 8] for g in range(0, ne, 8)], ne)
        solved.append(jnp.concatenate(rows, axis=0)[:, ne:])
    flipped = jnp.concatenate(solved, axis=0).T.astype(jnp.bfloat16)
    for to in range(nm):
        coeff[to] = flipped[to * half : (to + 1) * half]
    gives = []
    for offset in range(1, nm):
        gives.append(
            pltpu.make_async_remote_copy(
                src_ref=coeff.at[lax.rem(m + offset, nm)], dst_ref=coeff.at[nm + m],
                send_sem=c_send.at[offset - 1], recv_sem=c_recv.at[offset - 1],
                device_id=core(offset), device_id_type=MESH,
            )
        )
        gives[-1].start()
    kept = flipped[:half]
    for to in range(1, nm):
        kept = jnp.where(m == to, flipped[to * half : (to + 1) * half], kept)
    coeff[nm + m] = kept
    for copy in gives:
        copy.wait()
    regions = []
    for owner in range(nm):
        held = coeff[nm + owner]
        regions += [held[:, i * ne : (i + 1) * ne] for i in range(nreg)]
    for b in range(blocks):
        chosen = regions[0]
        for r in range(1, NLOC):
            chosen = jnp.where(region_ref[b] == r, regions[r], chosen)
        part = slice(b * BLOCK, (b + 1) * BLOCK)
        delta = jnp.dot(chosen, anomaly[:, part], preferred_element_type=jnp.float32)
        out_ref[:, part] = (members[:, part].astype(jnp.float32) + delta).astype(jnp.bfloat16)


def body(nz, nx, nm, members, observed, obs_error, obs_cells, perturbations, region_ids):
    half, width = members.shape
    count = observed.shape[0]
    ne = half * nm
    rows = NLOC // nm * ne
    chips = nz * nx
    vmem = pl.BlockSpec(memory_space=pltpu.VMEM)
    dma = pltpu.SemaphoreType.DMA
    return pl.pallas_call(
        functools.partial(kernel, nz, nx, nm),
        out_shape=jax.ShapeDtypeStruct(members.shape, members.dtype),
        in_specs=[pl.BlockSpec(memory_space=pltpu.SMEM)] + [vmem] * 5,
        out_specs=vmem,
        scratch_shapes=[
            pltpu.VMEM((ne, count), jnp.bfloat16),
            pltpu.VMEM((ne, width), jnp.bfloat16),
            pltpu.VMEM((rows, 2 * ne), jnp.bfloat16),
            pltpu.VMEM((chips - 1, rows, 2 * ne), jnp.bfloat16),
            pltpu.VMEM((2 * nm, half, rows), jnp.bfloat16),
            dma((nm - 1,)), dma((nm - 1,)), dma((nm - 1,)), dma((nm - 1,)),
            dma((chips - 1,)), dma((chips - 1,)), dma((nm - 1,)), dma((nm - 1,)),
        ],
        compiler_params=pltpu.CompilerParams(collective_id=0, has_side_effects=True),
    )(
        region_ids, members, observed.reshape(1, count), obs_error.reshape(1, count),
        obs_cells.reshape(1, count), perturbations,
    )


def solution(mesh):
    split = ("groups", "cells", "obs")
    in_specs = (P("mem", split), P(split), P(split), P(split), P(split, None), P(split))
    sizes = (mesh.shape["cells"], mesh.shape["obs"], mesh.shape["mem"])
    return jax.shard_map(
        functools.partial(body, *sizes), mesh=mesh, in_specs=in_specs, out_specs=P("mem", split), check_vma=False
    )
```

```python
import functools

import jax
import jax.numpy as jnp
from jax import lax
from jax.experimental import pallas as pl
from jax.experimental.pallas import tpu as pltpu
from jax.sharding import PartitionSpec as P

BLOCK = 512
NLOC = 4
LANE = 128
NE_GROUPS = 4
MESH = pl.DeviceIdType.MESH


def gather_lanes(table, cells):
    rows, width = table.shape
    columns = []
    for start in range(0, cells.shape[1], LANE):
        index = cells[:, start : start + LANE]
        low = jnp.broadcast_to(index % LANE, (rows, LANE))
        high = jnp.broadcast_to(index // LANE, (rows, LANE))
        total = None
        for part in range(width // LANE):
            found = jnp.take_along_axis(
                table[:, part * LANE : (part + 1) * LANE], low, axis=1, mode="promise_in_bounds"
            )
            total = found if total is None else jnp.where(high == part, found, total)
        columns.append(total)
    return jnp.concatenate(columns, axis=1)


def eliminate(rows, ne):
    groups = len(rows)
    sub = lax.broadcasted_iota(jnp.int32, rows[0].shape, 0)
    for block in range(groups):
        base = block * 8
        cols = [
            [jnp.broadcast_to(rows[g][:, base + j : base + j + 1], rows[g].shape) for g in range(groups)]
            for j in range(8)
        ]
        for j in range(8):
            inv = 1.0 / cols[j][block][j : j + 1, :]
            here = sub == j
            for l in range(j + 1, 8):
                factor = cols[l][block][j : j + 1, :] * inv
                for g in range(groups):
                    new = cols[l][g] - cols[j][g] * factor
                    cols[l][g] = jnp.where(here, factor, new) if g == block else new
            pivot_row = rows[block][j : j + 1, :] * inv
            for g in range(groups):
                new = rows[g] - cols[j][g] * pivot_row
                rows[g] = jnp.where(here, pivot_row, new) if g == block else new
    return rows


def kernel(
    nz, nx, nm, region_ref, members_ref, observed_ref, error_ref, cells_ref, noise_ref, out_ref,
    vals, whole, mine, slots, give, coeff,
    v_send, v_recv, w_send, w_recv, g_send, g_recv, c_send, c_recv,
):
    z, x, m = lax.axis_index("cells"), lax.axis_index("obs"), lax.axis_index("mem")
    half = members_ref.shape[0]
    ne = half * nm
    nreg = NLOC // nm
    chips = nz * nx
    blocks = region_ref.shape[0]

    groups = NE_GROUPS
    cols = ne // groups
    slices = nreg * groups
    here = z * nx + x
    slice_id = lax.rem(here, slices)

    def device(index, core):
        return {"cells": index // nx, "obs": lax.rem(index, nx), "mem": core}

    def chip(offset):
        return lax.rem(here + offset, chips)

    def core(offset):
        return lax.rem(m + offset, nm)

    barrier = pltpu.get_barrier_semaphore()
    for offset in range(chips):
        for step in range(nm):
            if offset or step:
                pl.semaphore_signal(
                    barrier, inc=1, device_id=device(chip(offset), core(step)), device_id_type=MESH
                )

    own = pl.ds(pl.multiple_of(m * half, half), half)
    cells = cells_ref[...]
    members = members_ref[...]
    vals[own, :] = gather_lanes(members.astype(jnp.float32), cells).astype(jnp.bfloat16)
    whole[own, :] = members
    block_of = cells // BLOCK
    region = jnp.full(cells.shape, region_ref[0], jnp.int32)
    for b in range(1, blocks):
        region = jnp.where(block_of == b, region_ref[b], region)
    weights = [jnp.where(region == m * nreg + i, 1.0, 0.0) for i in range(nreg)]
    inverse = 1.0 / error_ref[...]
    observed = observed_ref[...]

    pl.semaphore_wait(barrier, chips * nm - 1)
    swaps = []
    for offset in range(1, nm):
        swaps.append(
            pltpu.make_async_remote_copy(
                src_ref=vals.at[own], dst_ref=vals.at[own],
                send_sem=v_send.at[offset - 1], recv_sem=v_recv.at[offset - 1],
                device_id=device(here, core(offset)), device_id_type=MESH,
            )
        )
        swaps[-1].start()
    fetches = []
    for offset in range(1, nm):
        fetches.append(
            pltpu.make_async_remote_copy(
                src_ref=members_ref, dst_ref=whole.at[own],
                send_sem=w_send.at[offset - 1], recv_sem=w_recv.at[offset - 1],
                device_id=device(here, core(offset)), device_id_type=MESH,
            )
        )
        fetches[-1].start()
    noise = noise_ref[...].astype(jnp.float32)
    for copy in swaps:
        copy.wait()
    values = vals[...].astype(jnp.float32)
    predicted = values + 0.2 * values * values * values
    pmean = jnp.sum(predicted, axis=0, keepdims=True) / ne
    sens = (predicted - pmean) * inverse
    innov = (observed - predicted) * inverse + noise
    square = jnp.sum(innov * innov, axis=0, keepdims=True)
    joined = jnp.concatenate([sens, innov], axis=0).astype(jnp.bfloat16)
    masked = jnp.concatenate([sens * weight for weight in weights], axis=0).astype(jnp.bfloat16)
    partial = lax.dot_general(
        masked, joined, (((1,), (1,)), ((), ())), preferred_element_type=jnp.float32
    )
    diagonal = (
        lax.broadcasted_iota(jnp.int32, (ne, 2 * ne), 0)
        == lax.broadcasted_iota(jnp.int32, (ne, 2 * ne), 1)
    )
    partial = partial + jnp.concatenate(
        [
            jnp.where(
                diagonal,
                jnp.sum(square * weight, axis=1, keepdims=True) / ne,
                0.0,
            )
            for weight in weights
        ],
        axis=0,
    )
    fold = ne // 2
    for i in range(nreg):
        block = partial[i * ne : (i + 1) * ne]
        top, bottom = block[:fold], block[fold:]
        for k in range(groups):
            at = ne + k * cols
            mine[k * nreg + i] = jnp.concatenate(
                [top[:, :ne], bottom[:, fold:ne], top[:, at : at + cols], bottom[:, at : at + cols]], axis=1
            ).astype(jnp.bfloat16)
    shares = []
    for offset in range(1, chips):
        shares.append(
            pltpu.make_async_remote_copy(
                src_ref=mine.at[lax.rem(chip(offset), slices)], dst_ref=slots.at[offset - 1],
                send_sem=g_send.at[offset - 1], recv_sem=g_recv.at[offset - 1],
                device_id=device(chip(offset), m), device_id_type=MESH,
            )
        )
        shares[-1].start()

    for copy in fetches:
        copy.wait()
    ensemble = whole[...].astype(jnp.float32)
    center = jnp.sum(ensemble, axis=0, keepdims=True) / ne
    anomaly = (ensemble - center).astype(jnp.bfloat16)

    total = mine[slice_id].astype(jnp.float32)
    for offset, copy in enumerate(shares):
        copy.wait()
        total = total + slots[offset].astype(jnp.float32)

    pad = jnp.zeros((fold, ne - cols), jnp.float32)
    corner = total[:, fold:ne]
    system = jnp.concatenate(
        [
            jnp.concatenate([total[:, :ne], total[:, 3 * fold : 3 * fold + cols], pad], axis=1),
            jnp.concatenate([corner.T, total[:, ne : 3 * fold], total[:, 3 * fold + cols :], pad], axis=1),
        ],
        axis=0,
    )
    system = system + jnp.where(diagonal, ne - 1.0, 0.0)
    rows = eliminate([system[g : g + 8] for g in range(0, ne, 8)], ne)
    flipped = jnp.concatenate(rows, axis=0).T[ne : ne + cols]
    give[...] = jnp.concatenate([flipped, jnp.zeros_like(flipped)], axis=1).astype(jnp.bfloat16)

    per_core = groups // nm
    group = slice_id // nreg
    taker = group // per_core
    place = coeff.at[
        m * nreg + lax.rem(slice_id, nreg), pl.ds(pl.multiple_of(lax.rem(group, per_core) * cols, cols), cols)
    ]
    source = m * (nreg * per_core) + lax.rem(slice_id, nreg * per_core)
    first = here - slice_id
    remote = [
        pltpu.make_async_remote_copy(
            src_ref=give, dst_ref=place, send_sem=c_send.at[offset], recv_sem=c_recv.at[source],
            device_id=device(first + lax.rem(slice_id + offset, slices), taker), device_id_type=MESH,
        )
        for offset in range(slices)
    ]
    for copy in remote[1:]:
        copy.start()

    @pl.when(taker == m)
    def _():
        pltpu.make_async_copy(give, place, c_recv.at[source]).start()

    @pl.when(taker != m)
    def _():
        remote[0].start()
        remote[0].wait_send()

    for copy in remote[1:]:
        copy.wait_send()
    for owner in range(NLOC * per_core):
        pltpu.make_async_copy(give, coeff.at[owner // per_core, pl.ds(0, cols)], c_recv.at[owner]).wait()
    regions = [coeff[r][:, :ne] for r in range(NLOC)]
    for b in range(blocks):
        chosen = regions[0]
        for r in range(1, NLOC):
            chosen = jnp.where(region_ref[b] == r, regions[r], chosen)
        part = slice(b * BLOCK, (b + 1) * BLOCK)
        delta = jnp.dot(chosen, anomaly[:, part], preferred_element_type=jnp.float32)
        out_ref[:, part] = (members[:, part].astype(jnp.float32) + delta).astype(jnp.bfloat16)


def body(nz, nx, nm, members, observed, obs_error, obs_cells, perturbations, region_ids):
    half, width = members.shape
    count = observed.shape[0]
    ne = half * nm
    slices = NLOC // nm * NE_GROUPS
    chips = nz * nx
    vmem = pl.BlockSpec(memory_space=pltpu.VMEM)
    dma = pltpu.SemaphoreType.DMA
    return pl.pallas_call(
        functools.partial(kernel, nz, nx, nm),
        out_shape=jax.ShapeDtypeStruct(members.shape, members.dtype),
        in_specs=[pl.BlockSpec(memory_space=pltpu.SMEM)] + [vmem] * 5,
        out_specs=vmem,
        scratch_shapes=[
            pltpu.VMEM((ne, count), jnp.bfloat16),
            pltpu.VMEM((ne, width), jnp.bfloat16),
            pltpu.VMEM((slices, ne // 2, 2 * ne), jnp.bfloat16),
            pltpu.VMEM((chips - 1, ne // 2, 2 * ne), jnp.bfloat16),
            pltpu.VMEM((ne // NE_GROUPS, 2 * ne), jnp.bfloat16),
            pltpu.VMEM((NLOC, half, 2 * ne), jnp.bfloat16),
            dma((nm - 1,)), dma((nm - 1,)), dma((nm - 1,)), dma((nm - 1,)),
            dma((chips - 1,)), dma((chips - 1,)), dma((slices,)), dma((NLOC * NE_GROUPS // nm,)),
        ],
        compiler_params=pltpu.CompilerParams(collective_id=0, has_side_effects=True),
    )(
        region_ids, members, observed.reshape(1, count), obs_error.reshape(1, count),
        obs_cells.reshape(1, count), perturbations.T,
    )


def solution(mesh):
    split = ("groups", "cells", "obs")
    in_specs = (P("mem", split), P(split), P(split), P(split), P(split, None), P(split))
    sizes = (mesh.shape["cells"], mesh.shape["obs"], mesh.shape["mem"])
    return jax.shard_map(
        functools.partial(body, *sizes), mesh=mesh, in_specs=in_specs, out_specs=P("mem", split), check_vma=False
    )
```

```python
import functools

import jax
import jax.numpy as jnp
from jax import lax
from jax.experimental import pallas as pl
from jax.experimental.pallas import tpu as pltpu
from jax.sharding import PartitionSpec as P

BLOCK = 512
NLOC = 4
LANE = 128
NE_GROUPS = 4
MESH = pl.DeviceIdType.MESH


def gather_lanes(table, cells):
    rows, width = table.shape
    columns = []
    for start in range(0, cells.shape[1], LANE):
        index = cells[:, start : start + LANE]
        low = jnp.broadcast_to(index % LANE, (rows, LANE))
        high = jnp.broadcast_to(index // LANE, (rows, LANE))
        total = None
        for part in range(width // LANE):
            found = jnp.take_along_axis(
                table[:, part * LANE : (part + 1) * LANE], low, axis=1, mode="promise_in_bounds"
            )
            total = found if total is None else jnp.where(high == part, found, total)
        columns.append(total)
    return jnp.concatenate(columns, axis=1)


def eliminate(rows, ne):
    groups = len(rows)
    sub = lax.broadcasted_iota(jnp.int32, rows[0].shape, 0)
    for block in range(groups):
        base = block * 8
        cols = [
            [jnp.broadcast_to(rows[g][:, base + j : base + j + 1], rows[g].shape) for g in range(groups)]
            for j in range(8)
        ]
        for j in range(8):
            inv = 1.0 / cols[j][block][j : j + 1, :]
            here = sub == j
            for l in range(j + 1, 8):
                factor = cols[l][block][j : j + 1, :] * inv
                for g in range(groups):
                    new = cols[l][g] - cols[j][g] * factor
                    cols[l][g] = jnp.where(here, factor, new) if g == block else new
            pivot_row = rows[block][j : j + 1, :] * inv
            for g in range(groups):
                new = rows[g] - cols[j][g] * pivot_row
                rows[g] = jnp.where(here, pivot_row, new) if g == block else new
    return rows


def kernel(
    nz, nx, nm, region_any, members_any, observed_any, error_any, cells_any, noise_any, out_ref,
    region_ref, observed_ref, error_ref, cells_ref, noise_ref, loads,
    vals, whole, mine, slots, give, coeff,
    v_send, v_recv, w_send, w_recv, g_send, g_recv, c_send, c_recv,
):
    z, x, m = lax.axis_index("cells"), lax.axis_index("obs"), lax.axis_index("mem")
    half = members_any.shape[0]
    ne = half * nm
    nreg = NLOC // nm
    chips = nz * nx
    blocks = region_any.shape[0]

    groups = NE_GROUPS
    cols = ne // groups
    slices = nreg * groups
    here = z * nx + x
    slice_id = lax.rem(here, slices)

    def device(index, core):
        return {"cells": index // nx, "obs": lax.rem(index, nx), "mem": core}

    def chip(offset):
        return lax.rem(here + offset, chips)

    def core(offset):
        return lax.rem(m + offset, nm)

    barrier = pltpu.get_barrier_semaphore()
    for offset in range(chips):
        for step in range(nm):
            if offset or step:
                pl.semaphore_signal(
                    barrier, inc=1, device_id=device(chip(offset), core(step)), device_id_type=MESH
                )

    own = pl.ds(pl.multiple_of(m * half, half), half)
    staged = [
        pltpu.make_async_copy(source, target, loads.at[i])
        for i, (source, target) in enumerate(
            [
                (cells_any, cells_ref), (members_any, whole.at[own]), (region_any, region_ref),
                (error_any, error_ref), (observed_any, observed_ref), (noise_any, noise_ref),
            ]
        )
    ]
    for copy in staged:
        copy.start()
    for copy in staged[:2]:
        copy.wait()
    cells = cells_ref[...]
    members = whole[own, :]
    vals[own, :] = gather_lanes(members.astype(jnp.float32), cells).astype(jnp.bfloat16)
    for copy in staged[2:]:
        copy.wait()
    block_of = cells // BLOCK
    region = jnp.full(cells.shape, region_ref[0], jnp.int32)
    for b in range(1, blocks):
        region = jnp.where(block_of == b, region_ref[b], region)
    weights = [jnp.where(region == m * nreg + i, 1.0, 0.0) for i in range(nreg)]
    inverse = 1.0 / error_ref[...]
    observed = observed_ref[...]

    pl.semaphore_wait(barrier, chips * nm - 1)
    swaps = []
    for offset in range(1, nm):
        swaps.append(
            pltpu.make_async_remote_copy(
                src_ref=vals.at[own], dst_ref=vals.at[own],
                send_sem=v_send.at[offset - 1], recv_sem=v_recv.at[offset - 1],
                device_id=device(here, core(offset)), device_id_type=MESH,
            )
        )
        swaps[-1].start()
    fetches = []
    for offset in range(1, nm):
        fetches.append(
            pltpu.make_async_remote_copy(
                src_ref=whole.at[own], dst_ref=whole.at[own],
                send_sem=w_send.at[offset - 1], recv_sem=w_recv.at[offset - 1],
                device_id=device(here, core(offset)), device_id_type=MESH,
            )
        )
        fetches[-1].start()
    noise = noise_ref[...].astype(jnp.float32)
    for copy in swaps:
        copy.wait()
    values = vals[...].astype(jnp.float32)
    predicted = values + 0.2 * values * values * values
    pmean = jnp.sum(predicted, axis=0, keepdims=True) / ne
    sens = (predicted - pmean) * inverse
    innov = (observed - predicted) * inverse + noise
    square = jnp.sum(innov * innov, axis=0, keepdims=True)
    joined = jnp.concatenate([sens, innov], axis=0).astype(jnp.bfloat16)
    masked = jnp.concatenate([sens * weight for weight in weights], axis=0).astype(jnp.bfloat16)
    partial = lax.dot_general(
        masked, joined, (((1,), (1,)), ((), ())), preferred_element_type=jnp.float32
    )
    diagonal = (
        lax.broadcasted_iota(jnp.int32, (ne, 2 * ne), 0)
        == lax.broadcasted_iota(jnp.int32, (ne, 2 * ne), 1)
    )
    partial = partial + jnp.concatenate(
        [
            jnp.where(
                diagonal,
                jnp.sum(square * weight, axis=1, keepdims=True) / ne,
                0.0,
            )
            for weight in weights
        ],
        axis=0,
    )
    fold = ne // 2
    for i in range(nreg):
        block = partial[i * ne : (i + 1) * ne]
        top, bottom = block[:fold], block[fold:]
        for k in range(groups):
            at = ne + k * cols
            mine[k * nreg + i] = jnp.concatenate(
                [top[:, :ne], bottom[:, fold:ne], top[:, at : at + cols], bottom[:, at : at + cols]], axis=1
            ).astype(jnp.bfloat16)
    shares = []
    for offset in range(1, chips):
        shares.append(
            pltpu.make_async_remote_copy(
                src_ref=mine.at[lax.rem(chip(offset), slices)], dst_ref=slots.at[offset - 1],
                send_sem=g_send.at[offset - 1], recv_sem=g_recv.at[offset - 1],
                device_id=device(chip(offset), m), device_id_type=MESH,
            )
        )
        shares[-1].start()

    for copy in fetches:
        copy.wait()
    ensemble = whole[...].astype(jnp.float32)
    center = jnp.sum(ensemble, axis=0, keepdims=True) / ne
    anomaly = (ensemble - center).astype(jnp.bfloat16)

    total = mine[slice_id].astype(jnp.float32)
    for offset, copy in enumerate(shares):
        copy.wait()
        total = total + slots[offset].astype(jnp.float32)

    pad = jnp.zeros((fold, ne - cols), jnp.float32)
    corner = total[:, fold:ne]
    system = jnp.concatenate(
        [
            jnp.concatenate([total[:, :ne], total[:, 3 * fold : 3 * fold + cols], pad], axis=1),
            jnp.concatenate([corner.T, total[:, ne : 3 * fold], total[:, 3 * fold + cols :], pad], axis=1),
        ],
        axis=0,
    )
    system = system + jnp.where(diagonal, ne - 1.0, 0.0)
    rows = eliminate([system[g : g + 8] for g in range(0, ne, 8)], ne)
    flipped = jnp.concatenate(rows, axis=0).T[ne : ne + cols]
    give[...] = jnp.concatenate([flipped, jnp.zeros_like(flipped)], axis=1).astype(jnp.bfloat16)

    per_core = groups // nm
    group = slice_id // nreg
    taker = group // per_core
    place = coeff.at[
        m * nreg + lax.rem(slice_id, nreg), pl.ds(pl.multiple_of(lax.rem(group, per_core) * cols, cols), cols)
    ]
    source = m * (nreg * per_core) + lax.rem(slice_id, nreg * per_core)
    first = here - slice_id
    remote = [
        pltpu.make_async_remote_copy(
            src_ref=give, dst_ref=place, send_sem=c_send.at[offset], recv_sem=c_recv.at[source],
            device_id=device(first + lax.rem(slice_id + offset, slices), taker), device_id_type=MESH,
        )
        for offset in range(slices)
    ]
    for copy in remote[1:]:
        copy.start()

    @pl.when(taker == m)
    def _():
        pltpu.make_async_copy(give, place, c_recv.at[source]).start()

    @pl.when(taker != m)
    def _():
        remote[0].start()
        remote[0].wait_send()

    for copy in remote[1:]:
        copy.wait_send()
    for owner in range(NLOC * per_core):
        pltpu.make_async_copy(give, coeff.at[owner // per_core, pl.ds(0, cols)], c_recv.at[owner]).wait()
    regions = [coeff[r][:, :ne] for r in range(NLOC)]
    for b in range(blocks):
        chosen = regions[0]
        for r in range(1, NLOC):
            chosen = jnp.where(region_ref[b] == r, regions[r], chosen)
        part = slice(b * BLOCK, (b + 1) * BLOCK)
        delta = jnp.dot(chosen, anomaly[:, part], preferred_element_type=jnp.float32)
        out_ref[:, part] = (members[:, part].astype(jnp.float32) + delta).astype(jnp.bfloat16)


def body(nz, nx, nm, members, observed, obs_error, obs_cells, perturbations, region_ids):
    half, width = members.shape
    count = observed.shape[0]
    ne = half * nm
    slices = NLOC // nm * NE_GROUPS
    chips = nz * nx
    vmem = pl.BlockSpec(memory_space=pltpu.VMEM)
    dma = pltpu.SemaphoreType.DMA
    return pl.pallas_call(
        functools.partial(kernel, nz, nx, nm),
        out_shape=pltpu.VMEM(members.shape, members.dtype),
        in_specs=[pl.BlockSpec(memory_space=pl.ANY)] * 6,
        out_specs=vmem,
        scratch_shapes=[
            pltpu.SMEM(region_ids.shape, jnp.int32),
            pltpu.VMEM((1, count), jnp.float32),
            pltpu.VMEM((1, count), jnp.float32),
            pltpu.VMEM((1, count), jnp.int32),
            pltpu.VMEM((ne, count), jnp.bfloat16),
            dma((6,)),
            pltpu.VMEM((ne, count), jnp.bfloat16),
            pltpu.VMEM((ne, width), jnp.bfloat16),
            pltpu.VMEM((slices, ne // 2, 2 * ne), jnp.bfloat16),
            pltpu.VMEM((chips - 1, ne // 2, 2 * ne), jnp.bfloat16),
            pltpu.VMEM((ne // NE_GROUPS, 2 * ne), jnp.bfloat16),
            pltpu.VMEM((NLOC, half, 2 * ne), jnp.bfloat16),
            dma((nm - 1,)), dma((nm - 1,)), dma((nm - 1,)), dma((nm - 1,)),
            dma((chips - 1,)), dma((chips - 1,)), dma((slices,)), dma((NLOC * NE_GROUPS // nm,)),
        ],
        compiler_params=pltpu.CompilerParams(collective_id=0, has_side_effects=True),
    )(
        region_ids, members, observed.reshape(1, count), obs_error.reshape(1, count),
        obs_cells.reshape(1, count), perturbations.T,
    )


def solution(mesh):
    split = ("groups", "cells", "obs")
    in_specs = (P("mem", split), P(split), P(split), P(split), P(split, None), P(split))
    sizes = (mesh.shape["cells"], mesh.shape["obs"], mesh.shape["mem"])
    return jax.shard_map(
        functools.partial(body, *sizes), mesh=mesh, in_specs=in_specs, out_specs=P("mem", split), check_vma=False
    )
```

```python
import functools

import jax
import jax.numpy as jnp
from jax import lax
from jax.experimental import pallas as pl
from jax.experimental.pallas import tpu as pltpu
from jax.sharding import PartitionSpec as P

BLOCK = 512
NLOC = 4
LANE = 128
MESH = pl.DeviceIdType.MESH


def gather_lanes(table, cells):
    rows, width = table.shape
    columns = []
    for start in range(0, cells.shape[1], LANE):
        index = cells[:, start : start + LANE]
        low = jnp.broadcast_to(index % LANE, (rows, LANE))
        high = jnp.broadcast_to(index // LANE, (rows, LANE))
        total = None
        for part in range(width // LANE):
            found = jnp.take_along_axis(
                table[:, part * LANE : (part + 1) * LANE], low, axis=1, mode="promise_in_bounds"
            )
            total = found if total is None else jnp.where(high == part, found, total)
        columns.append(total)
    return jnp.concatenate(columns, axis=1)


def eliminate(rows, ne):
    groups = len(rows)
    sub = lax.broadcasted_iota(jnp.int32, rows[0].shape, 0)
    for block in range(groups):
        base = block * 8
        cols = [
            [jnp.broadcast_to(rows[g][:, base + j : base + j + 1], rows[g].shape) for g in range(groups)]
            for j in range(8)
        ]
        for j in range(8):
            inv = 1.0 / cols[j][block][j : j + 1, :]
            here = sub == j
            for l in range(j + 1, 8):
                factor = cols[l][block][j : j + 1, :] * inv
                for g in range(groups):
                    new = cols[l][g] - cols[j][g] * factor
                    cols[l][g] = jnp.where(here, factor, new) if g == block else new
            pivot_row = rows[block][j : j + 1, :] * inv
            for g in range(groups):
                new = rows[g] - cols[j][g] * pivot_row
                rows[g] = jnp.where(here, pivot_row, new) if g == block else new
    return rows


def kernel(
    nz, nx, nm, region_any, members_any, observed_any, error_any, cells_any, noise_any, out_ref,
    region_ref, observed_ref, error_ref, cells_ref, noise_ref, loads,
    vals, whole, mine, slots, give, coeff,
    v_send, v_recv, w_send, w_recv, g_send, g_recv, c_send, c_recv,
):
    z, x, m = lax.axis_index("cells"), lax.axis_index("obs"), lax.axis_index("mem")
    half = members_any.shape[0]
    ne = half * nm
    nreg = NLOC // nm
    chips = nz * nx
    blocks = region_any.shape[0]

    slices = nreg
    here = z * nx + x
    slice_id = lax.rem(here, slices)

    def device(index, core):
        return {"cells": index // nx, "obs": lax.rem(index, nx), "mem": core}

    def chip(offset):
        return lax.rem(here + offset, chips)

    def core(offset):
        return lax.rem(m + offset, nm)

    barrier = pltpu.get_barrier_semaphore()
    for offset in range(chips):
        for step in range(nm):
            if offset or step:
                pl.semaphore_signal(
                    barrier, inc=1, device_id=device(chip(offset), core(step)), device_id_type=MESH
                )

    own = pl.ds(pl.multiple_of(m * half, half), half)
    staged = [
        pltpu.make_async_copy(source, target, loads.at[i])
        for i, (source, target) in enumerate(
            [
                (cells_any, cells_ref), (members_any, whole.at[own]), (region_any, region_ref),
                (error_any, error_ref), (observed_any, observed_ref), (noise_any, noise_ref),
            ]
        )
    ]
    for copy in staged:
        copy.start()
    for copy in staged[:2]:
        copy.wait()
    cells = cells_ref[...]
    members = whole[own, :]
    vals[own, :] = gather_lanes(members.astype(jnp.float32), cells).astype(jnp.bfloat16)
    for copy in staged[2:]:
        copy.wait()
    block_of = cells // BLOCK
    region = jnp.full(cells.shape, region_ref[0], jnp.int32)
    for b in range(1, blocks):
        region = jnp.where(block_of == b, region_ref[b], region)
    weights = [jnp.where(region == m * nreg + i, 1.0, 0.0) for i in range(nreg)]
    inverse = 1.0 / error_ref[...]
    observed = observed_ref[...]

    pl.semaphore_wait(barrier, chips * nm - 1)
    swaps = []
    for offset in range(1, nm):
        swaps.append(
            pltpu.make_async_remote_copy(
                src_ref=vals.at[own], dst_ref=vals.at[own],
                send_sem=v_send.at[offset - 1], recv_sem=v_recv.at[offset - 1],
                device_id=device(here, core(offset)), device_id_type=MESH,
            )
        )
        swaps[-1].start()
    fetches = []
    for offset in range(1, nm):
        fetches.append(
            pltpu.make_async_remote_copy(
                src_ref=whole.at[own], dst_ref=whole.at[own],
                send_sem=w_send.at[offset - 1], recv_sem=w_recv.at[offset - 1],
                device_id=device(here, core(offset)), device_id_type=MESH,
            )
        )
        fetches[-1].start()
    noise = noise_ref[...].astype(jnp.float32)
    for copy in swaps:
        copy.wait()
    values = vals[...].astype(jnp.float32)
    predicted = values + 0.2 * values * values * values
    pmean = jnp.sum(predicted, axis=0, keepdims=True) / ne
    sens = (predicted - pmean) * inverse
    innov = (observed - predicted) * inverse + noise
    square = jnp.sum(innov * innov, axis=0, keepdims=True)
    joined = jnp.concatenate([sens, innov], axis=0).astype(jnp.bfloat16)
    masked = jnp.concatenate([sens * weight for weight in weights], axis=0).astype(jnp.bfloat16)
    partial = lax.dot_general(
        masked, joined, (((1,), (1,)), ((), ())), preferred_element_type=jnp.float32
    )
    diagonal = (
        lax.broadcasted_iota(jnp.int32, (ne, 2 * ne), 0)
        == lax.broadcasted_iota(jnp.int32, (ne, 2 * ne), 1)
    )
    partial = partial + jnp.concatenate(
        [
            jnp.where(
                diagonal,
                jnp.sum(square * weight, axis=1, keepdims=True) / ne,
                0.0,
            )
            for weight in weights
        ],
        axis=0,
    )
    for i in range(nreg):
        mine[i] = partial[i * ne : (i + 1) * ne].astype(jnp.bfloat16)
    shares = []
    for offset in range(1, chips):
        shares.append(
            pltpu.make_async_remote_copy(
                src_ref=mine.at[lax.rem(chip(offset), slices)], dst_ref=slots.at[offset - 1],
                send_sem=g_send.at[offset - 1], recv_sem=g_recv.at[offset - 1],
                device_id=device(chip(offset), m), device_id_type=MESH,
            )
        )
        shares[-1].start()

    for copy in fetches:
        copy.wait()
    ensemble = whole[...].astype(jnp.float32)
    center = jnp.sum(ensemble, axis=0, keepdims=True) / ne
    anomaly = (ensemble - center).astype(jnp.bfloat16)

    total = mine[slice_id].astype(jnp.float32)
    for offset, copy in enumerate(shares):
        copy.wait()
        total = total + slots[offset].astype(jnp.float32)

    system = total + jnp.where(diagonal, ne - 1.0, 0.0)
    rows = eliminate([system[g : g + 8] for g in range(0, ne, 8)], ne)
    flipped = jnp.concatenate(rows, axis=0).T[ne:]
    give[...] = jnp.concatenate([flipped, jnp.zeros_like(flipped)], axis=1).astype(jnp.bfloat16)

    owned = m * nreg + slice_id
    gifts = []
    for offset in range(slices):
        for step in range(nm):
            if offset or step:
                gifts.append(
                    pltpu.make_async_remote_copy(
                        src_ref=give.at[pl.ds(pl.multiple_of(core(step) * half, half), half)],
                        dst_ref=coeff.at[owned],
                        send_sem=c_send.at[offset * nm + step], recv_sem=c_recv.at[owned],
                        device_id=device(here - slice_id + lax.rem(slice_id + offset, slices), core(step)),
                        device_id_type=MESH,
                    )
                )
                gifts[-1].start()
    pltpu.make_async_copy(give.at[own], coeff.at[owned], c_recv.at[owned]).start()
    for copy in gifts:
        copy.wait_send()
    for r in range(NLOC):
        pltpu.make_async_copy(give.at[pl.ds(0, half)], coeff.at[r], c_recv.at[r]).wait()
    regions = [coeff[r][:, :ne] for r in range(NLOC)]
    for b in range(blocks):
        chosen = regions[0]
        for r in range(1, NLOC):
            chosen = jnp.where(region_ref[b] == r, regions[r], chosen)
        part = slice(b * BLOCK, (b + 1) * BLOCK)
        delta = jnp.dot(chosen, anomaly[:, part], preferred_element_type=jnp.float32)
        out_ref[:, part] = (members[:, part].astype(jnp.float32) + delta).astype(jnp.bfloat16)


def body(nz, nx, nm, members, observed, obs_error, obs_cells, perturbations, region_ids):
    half, width = members.shape
    count = observed.shape[0]
    ne = half * nm
    slices = NLOC // nm
    chips = nz * nx
    vmem = pl.BlockSpec(memory_space=pltpu.VMEM)
    dma = pltpu.SemaphoreType.DMA
    return pl.pallas_call(
        functools.partial(kernel, nz, nx, nm),
        out_shape=pltpu.VMEM(members.shape, members.dtype),
        in_specs=[pl.BlockSpec(memory_space=pl.ANY)] * 6,
        out_specs=vmem,
        scratch_shapes=[
            pltpu.SMEM(region_ids.shape, jnp.int32),
            pltpu.VMEM((1, count), jnp.float32),
            pltpu.VMEM((1, count), jnp.float32),
            pltpu.VMEM((1, count), jnp.int32),
            pltpu.VMEM((ne, count), jnp.bfloat16),
            dma((6,)),
            pltpu.VMEM((ne, count), jnp.bfloat16),
            pltpu.VMEM((ne, width), jnp.bfloat16),
            pltpu.VMEM((slices, ne, 2 * ne), jnp.bfloat16),
            pltpu.VMEM((chips - 1, ne, 2 * ne), jnp.bfloat16),
            pltpu.VMEM((ne, 2 * ne), jnp.bfloat16),
            pltpu.VMEM((NLOC, half, 2 * ne), jnp.bfloat16),
            dma((nm - 1,)), dma((nm - 1,)), dma((nm - 1,)), dma((nm - 1,)),
            dma((chips - 1,)), dma((chips - 1,)), dma((slices * nm,)), dma((NLOC,)),
        ],
        compiler_params=pltpu.CompilerParams(collective_id=0, has_side_effects=True),
    )(
        region_ids, members, observed.reshape(1, count), obs_error.reshape(1, count),
        obs_cells.reshape(1, count), perturbations.T,
    )


def solution(mesh):
    split = ("groups", "cells", "obs")
    in_specs = (P("mem", split), P(split), P(split), P(split), P(split, None), P(split))
    sizes = (mesh.shape["cells"], mesh.shape["obs"], mesh.shape["mem"])
    return jax.shard_map(
        functools.partial(body, *sizes), mesh=mesh, in_specs=in_specs, out_specs=P("mem", split), check_vma=False
    )
```

```python
import functools

import jax
import jax.numpy as jnp
from jax import lax
from jax.experimental import pallas as pl
from jax.experimental.pallas import tpu as pltpu
from jax.sharding import PartitionSpec as P

BLOCK = 512
NLOC = 4
LANE = 128
MESH = pl.DeviceIdType.MESH


def gather_lanes(table, cells):
    rows, width = table.shape
    columns = []
    for start in range(0, cells.shape[1], LANE):
        index = cells[:, start : start + LANE]
        low = jnp.broadcast_to(index % LANE, (rows, LANE))
        high = jnp.broadcast_to(index // LANE, (rows, LANE))
        total = None
        for part in range(width // LANE):
            found = jnp.take_along_axis(
                table[:, part * LANE : (part + 1) * LANE], low, axis=1, mode="promise_in_bounds"
            )
            total = found if total is None else jnp.where(high == part, found, total)
        columns.append(total)
    return jnp.concatenate(columns, axis=1)


def eliminate(rows, ne):
    groups = len(rows)
    sub = lax.broadcasted_iota(jnp.int32, rows[0].shape, 0)
    width = 4
    for base in range(0, ne, width):
        block, first = base // 8, base % 8
        cols = [
            [jnp.broadcast_to(rows[g][:, base + j : base + j + 1], rows[g].shape) for g in range(groups)]
            for j in range(width)
        ]
        for j in range(width):
            at = first + j
            inv = 1.0 / cols[j][block][at : at + 1, :]
            here = sub == at
            for l in range(j + 1, width):
                factor = cols[l][block][at : at + 1, :] * inv
                for g in range(groups):
                    new = cols[l][g] - cols[j][g] * factor
                    cols[l][g] = jnp.where(here, factor, new) if g == block else new
            pivot_row = rows[block][at : at + 1, :] * inv
            for g in range(groups):
                new = rows[g] - cols[j][g] * pivot_row
                rows[g] = jnp.where(here, pivot_row, new) if g == block else new
    return rows


def kernel(
    nz, nx, nm, region_any, members_any, observed_any, error_any, cells_any, noise_any, out_ref,
    region_ref, observed_ref, error_ref, cells_ref, noise_ref, loads,
    vals, whole, mine, slots, give, coeff,
    v_send, v_recv, w_send, w_recv, g_send, g_recv, c_send, c_recv,
):
    z, x, m = lax.axis_index("cells"), lax.axis_index("obs"), lax.axis_index("mem")
    half = members_any.shape[0]
    ne = half * nm
    nreg = NLOC // nm
    chips = nz * nx
    blocks = region_any.shape[0]

    slices = nreg
    here = z * nx + x
    slice_id = lax.rem(here, slices)

    def device(index, core):
        return {"cells": index // nx, "obs": lax.rem(index, nx), "mem": core}

    def chip(offset):
        return lax.rem(here + offset, chips)

    def core(offset):
        return lax.rem(m + offset, nm)

    barrier = pltpu.get_barrier_semaphore()
    for offset in range(chips):
        for step in range(nm):
            if offset or step:
                pl.semaphore_signal(
                    barrier, inc=1, device_id=device(chip(offset), core(step)), device_id_type=MESH
                )

    own = pl.ds(pl.multiple_of(m * half, half), half)
    staged = [
        pltpu.make_async_copy(source, target, loads.at[i])
        for i, (source, target) in enumerate(
            [
                (cells_any, cells_ref), (members_any, whole.at[own]), (region_any, region_ref),
                (error_any, error_ref), (observed_any, observed_ref), (noise_any, noise_ref),
            ]
        )
    ]
    for copy in staged:
        copy.start()
    for copy in staged[:2]:
        copy.wait()
    cells = cells_ref[...]
    members = whole[own, :]
    vals[own, :] = gather_lanes(members.astype(jnp.float32), cells).astype(jnp.bfloat16)
    for copy in staged[2:]:
        copy.wait()
    block_of = cells // BLOCK
    region = jnp.full(cells.shape, region_ref[0], jnp.int32)
    for b in range(1, blocks):
        region = jnp.where(block_of == b, region_ref[b], region)
    weights = [jnp.where(region == m * nreg + i, 1.0, 0.0) for i in range(nreg)]
    inverse = 1.0 / error_ref[...]
    observed = observed_ref[...]

    pl.semaphore_wait(barrier, chips * nm - 1)
    swaps = []
    for offset in range(1, nm):
        swaps.append(
            pltpu.make_async_remote_copy(
                src_ref=vals.at[own], dst_ref=vals.at[own],
                send_sem=v_send.at[offset - 1], recv_sem=v_recv.at[offset - 1],
                device_id=device(here, core(offset)), device_id_type=MESH,
            )
        )
        swaps[-1].start()
    fetches = []
    for offset in range(1, nm):
        fetches.append(
            pltpu.make_async_remote_copy(
                src_ref=whole.at[own], dst_ref=whole.at[own],
                send_sem=w_send.at[offset - 1], recv_sem=w_recv.at[offset - 1],
                device_id=device(here, core(offset)), device_id_type=MESH,
            )
        )
        fetches[-1].start()
    noise = noise_ref[...].astype(jnp.float32)
    for copy in swaps:
        copy.wait()
    values = vals[...].astype(jnp.float32)
    predicted = values + 0.2 * values * values * values
    pmean = jnp.sum(predicted, axis=0, keepdims=True) / ne
    sens = (predicted - pmean) * inverse
    innov = (observed - predicted) * inverse + noise
    square = jnp.sum(innov * innov, axis=0, keepdims=True)
    joined = jnp.concatenate([sens, innov], axis=0).astype(jnp.bfloat16)
    masked = jnp.concatenate([sens * weight for weight in weights], axis=0).astype(jnp.bfloat16)
    partial = lax.dot_general(
        masked, joined, (((1,), (1,)), ((), ())), preferred_element_type=jnp.float32
    )
    diagonal = (
        lax.broadcasted_iota(jnp.int32, (ne, 2 * ne), 0)
        == lax.broadcasted_iota(jnp.int32, (ne, 2 * ne), 1)
    )
    partial = partial + jnp.concatenate(
        [
            jnp.where(
                diagonal,
                jnp.sum(square * weight, axis=1, keepdims=True) / ne,
                0.0,
            )
            for weight in weights
        ],
        axis=0,
    )
    for i in range(nreg):
        mine[i] = partial[i * ne : (i + 1) * ne].astype(jnp.bfloat16)
    shares = []
    for offset in range(1, chips):
        shares.append(
            pltpu.make_async_remote_copy(
                src_ref=mine.at[lax.rem(chip(offset), slices)], dst_ref=slots.at[offset - 1],
                send_sem=g_send.at[offset - 1], recv_sem=g_recv.at[offset - 1],
                device_id=device(chip(offset), m), device_id_type=MESH,
            )
        )
        shares[-1].start()

    for copy in fetches:
        copy.wait()
    ensemble = whole[...].astype(jnp.float32)
    center = jnp.sum(ensemble, axis=0, keepdims=True) / ne
    anomaly = (ensemble - center).astype(jnp.bfloat16)

    total = mine[slice_id].astype(jnp.float32)
    for offset, copy in enumerate(shares):
        copy.wait()
        total = total + slots[offset].astype(jnp.float32)

    system = total + jnp.where(diagonal, ne - 1.0, 0.0)
    rows = eliminate([system[g : g + 8] for g in range(0, ne, 8)], ne)
    flipped = jnp.concatenate(rows, axis=0).T[ne:]
    give[...] = jnp.concatenate([flipped, jnp.zeros_like(flipped)], axis=1).astype(jnp.bfloat16)

    owned = m * nreg + slice_id
    gifts = []
    for offset in range(slices):
        for step in range(nm):
            if offset or step:
                gifts.append(
                    pltpu.make_async_remote_copy(
                        src_ref=give.at[pl.ds(pl.multiple_of(core(step) * half, half), half)],
                        dst_ref=coeff.at[owned],
                        send_sem=c_send.at[offset * nm + step], recv_sem=c_recv.at[owned],
                        device_id=device(here - slice_id + lax.rem(slice_id + offset, slices), core(step)),
                        device_id_type=MESH,
                    )
                )
                gifts[-1].start()
    pltpu.make_async_copy(give.at[own], coeff.at[owned], c_recv.at[owned]).start()
    for copy in gifts:
        copy.wait_send()
    for r in range(NLOC):
        pltpu.make_async_copy(give.at[pl.ds(0, half)], coeff.at[r], c_recv.at[r]).wait()
    regions = [coeff[r][:, :ne] for r in range(NLOC)]
    for b in range(blocks):
        chosen = regions[0]
        for r in range(1, NLOC):
            chosen = jnp.where(region_ref[b] == r, regions[r], chosen)
        part = slice(b * BLOCK, (b + 1) * BLOCK)
        delta = jnp.dot(chosen, anomaly[:, part], preferred_element_type=jnp.float32)
        out_ref[:, part] = (members[:, part].astype(jnp.float32) + delta).astype(jnp.bfloat16)


def body(nz, nx, nm, members, observed, obs_error, obs_cells, perturbations, region_ids):
    half, width = members.shape
    count = observed.shape[0]
    ne = half * nm
    slices = NLOC // nm
    chips = nz * nx
    vmem = pl.BlockSpec(memory_space=pltpu.VMEM)
    dma = pltpu.SemaphoreType.DMA
    return pl.pallas_call(
        functools.partial(kernel, nz, nx, nm),
        out_shape=pltpu.VMEM(members.shape, members.dtype),
        in_specs=[pl.BlockSpec(memory_space=pl.ANY)] * 6,
        out_specs=vmem,
        scratch_shapes=[
            pltpu.SMEM(region_ids.shape, jnp.int32),
            pltpu.VMEM((1, count), jnp.float32),
            pltpu.VMEM((1, count), jnp.float32),
            pltpu.VMEM((1, count), jnp.int32),
            pltpu.VMEM((ne, count), jnp.bfloat16),
            dma((6,)),
            pltpu.VMEM((ne, count), jnp.bfloat16),
            pltpu.VMEM((ne, width), jnp.bfloat16),
            pltpu.VMEM((slices, ne, 2 * ne), jnp.bfloat16),
            pltpu.VMEM((chips - 1, ne, 2 * ne), jnp.bfloat16),
            pltpu.VMEM((ne, 2 * ne), jnp.bfloat16),
            pltpu.VMEM((NLOC, half, 2 * ne), jnp.bfloat16),
            dma((nm - 1,)), dma((nm - 1,)), dma((nm - 1,)), dma((nm - 1,)),
            dma((chips - 1,)), dma((chips - 1,)), dma((slices * nm,)), dma((NLOC,)),
        ],
        compiler_params=pltpu.CompilerParams(collective_id=0, has_side_effects=True),
    )(
        region_ids, members, observed.reshape(1, count), obs_error.reshape(1, count),
        obs_cells.reshape(1, count), perturbations.T,
    )


def solution(mesh):
    split = ("groups", "cells", "obs")
    in_specs = (P("mem", split), P(split), P(split), P(split), P(split, None), P(split))
    sizes = (mesh.shape["cells"], mesh.shape["obs"], mesh.shape["mem"])
    return jax.shard_map(
        functools.partial(body, *sizes), mesh=mesh, in_specs=in_specs, out_specs=P("mem", split), check_vma=False
    )
```
